32 devices in a mesh: team: 4 (over z), blk: 4 (over y, x), head: 2 (over core).
Axes of the slice: x: 2, y: 2, z: 4, core: 2. Of those that a mesh axis runs over, the one named last changes fastest.
Arguments:
- query: bfloat16 [2048, 2560], P(('team', 'blk'), 'head'), parts along dimension 1, may hold values from -15 to 15
- keys: bfloat16 [2048, 2560], P(('team', 'blk'), 'head'), parts along dimension 1, may hold values from -6 to 6
- values: bfloat16 [2048, 2560], P(('team', 'blk'), 'head'), parts along dimension 1, may hold values from -6 to 6
Outputs:
- attended: bfloat16 [2048, 2560], P(('team', 'blk'), 'head'), parts along dimension 1
The draws below stay inside these ranges and needn't reach their ends.
There are 2 independent parts, one for each index of `head`. The reference program is written for one: setup_inputs(seed, part) draws one part's arguments, and reference() takes and returns one part's arrays. A program takes and returns all parts, laid end to end along the dimension named above; each array names one. Nothing has to cross between parts.
All inputs are finite; a program needn't handle non-finite values.
Results may differ from the reference program's by a relative error of at most 0.006.
Values may be sent and summed in bfloat16 or wider, within the bound.
A program may use at most 128 MiB of HBM per device.

```python
import math
import jax
import jax.numpy as jnp
from jax import lax

HEADS = 10
HEAD_DIM = 128
TOKENS = 2048


def paired_draw(key):
    query_key = jax.random.fold_in(key, 11)
    keys_key = jax.random.fold_in(key, 12)
    shape = (TOKENS, HEADS * HEAD_DIM)
    query = jnp.clip(2.5 * jax.random.normal(query_key, shape, jnp.float32), -15.0, 15.0)
    keys = jnp.clip(jax.random.normal(keys_key, shape, jnp.float32), -6.0, 6.0)
    return (query, keys)


def draw_query(key, part):
    return paired_draw(key)[0].astype(jnp.bfloat16)


def draw_keys(key, part):
    return paired_draw(key)[1].astype(jnp.bfloat16)


def block_scale(key, shape, split, least, largest):
    level = 1.0
    for dim, shards_of in split:
        draws = jax.random.uniform(jax.random.fold_in(jax.random.fold_in(key, 6), dim), (shards_of,), jnp.float32, least / len(split), largest / len(split))
        level = level * jnp.repeat(jnp.exp(draws), shape[dim] // shards_of).reshape((-1,) + (1,) * (len(shape) - 1 - dim))
    return level


def bell_draw(stream_key, shape, width, bound, pieces=(), kind=jnp.bfloat16):
    array = width * jax.random.normal(stream_key, shape, jnp.float32)
    if pieces:
        array = array * block_scale(stream_key, shape, pieces, -0.22, 0.18)
    return jnp.clip(array, -bound, bound).astype(kind)


def setup_inputs(seed: int = 0, part: int = 0) -> dict:
    streams_of = jax.random.split(jax.random.key(seed), 4)
    part_keys = jax.random.split(jax.random.fold_in(streams_of[3], part), 4)
    return {
        "query": draw_query(jax.random.fold_in(jax.random.fold_in(streams_of[3], part), 71), part),
        "keys": draw_keys(jax.random.fold_in(jax.random.fold_in(streams_of[3], part), 71), part),
        "values": bell_draw(part_keys[2], (TOKENS, HEADS * HEAD_DIM), 1.0, 6.0, ((0, 16),)),
    }


def attend_rows(query_block, key_head, value_head):
    score_scale = 1.0 / math.sqrt(HEAD_DIM)
    scores = jnp.dot(query_block, key_head.T, preferred_element_type=jnp.float32) * score_scale
    peak = lax.optimization_barrier(jnp.max(scores, axis=1, keepdims=True))
    raised = jnp.exp(scores - peak)
    denominator = lax.optimization_barrier(jnp.sum(raised, axis=1, keepdims=True))
    weights = raised.astype(jnp.bfloat16)
    summed = jnp.dot(weights, value_head, preferred_element_type=jnp.float32)
    return (summed / denominator).astype(jnp.bfloat16)

def reference(query, keys, values):
    token_count = query.shape[0]
    block_rows = math.gcd(token_count, 512)
    query_heads = query.reshape(token_count, HEADS, HEAD_DIM).transpose(1, 0, 2)
    key_heads = keys.reshape(token_count, HEADS, HEAD_DIM).transpose(1, 0, 2)
    value_heads = values.reshape(token_count, HEADS, HEAD_DIM).transpose(1, 0, 2)

    def one_head(triple):
        query_head, key_head, value_head = triple
        blocks = query_head.reshape(token_count // block_rows, block_rows, HEAD_DIM)
        result = lax.map(lambda block: attend_rows(block, key_head, value_head), blocks)
        return result.reshape(token_count, HEAD_DIM)
    outputs = lax.map(one_head, (query_heads, key_heads, value_heads))
    return outputs.transpose(1, 0, 2).reshape(token_count, HEADS * HEAD_DIM)
```

```python
import functools
import math

import jax
import jax.numpy as jnp
from jax import lax
from jax.experimental import pallas as pl
from jax.experimental.pallas import tpu as pltpu
from jax.sharding import PartitionSpec as P

HEAD_DIM = 128
MESH = pl.DeviceIdType.MESH
RIGHT, LEFT = 0, 1


def merge(o1, s1, o2, s2):
    top = jnp.maximum(s1, s2)
    a1 = jnp.exp2(s1 - top)
    a2 = jnp.exp2(s2 - top)
    total = a1 + a2
    inverse = 1.0 / total
    return o1 * (a1 * inverse) + o2 * (a2 * inverse), top + jnp.log2(total)


def kernel(
    team, blk, q_ref, k_ref, v_ref, out_ref,
    qbuf, kvbuf, part_o, part_s, o_in, s_in, o_out, s_out,
    q_recv, q_send, kv_recv, kv_send, o_recv, o_send, s_recv, s_send,
):
    rows = q_ref.shape[0]
    heads = q_ref.shape[1] // HEAD_DIM
    scale = math.log2(math.e) / math.sqrt(HEAD_DIM)
    t = lax.axis_index("team")
    b = lax.axis_index("blk")
    last = team - 1

    def columns(h):
        return pl.ds(pl.multiple_of(h * HEAD_DIM, HEAD_DIM), HEAD_DIM)

    barrier = pltpu.get_barrier_semaphore()

    @pl.loop(1, blk)
    def _(r):
        pl.semaphore_signal(
            barrier, inc=1, device_id={"blk": lax.rem(b + r, blk)}, device_id_type=MESH
        )

    @pl.when(t > 0)
    def _():
        pl.semaphore_signal(barrier, inc=1, device_id={"team": t - 1}, device_id_type=MESH)

    @pl.when(t < last)
    def _():
        pl.semaphore_signal(barrier, inc=1, device_id={"team": t + 1}, device_id_type=MESH)

    ends = jnp.where(t > 0, 1, 0) + jnp.where(t < last, 1, 0)
    pl.semaphore_wait(barrier, blk - 1 + ends)

    def kv_copy(h, which, r):
        source = (k_ref, v_ref)[which]
        return pltpu.make_async_remote_copy(
            src_ref=source.at[:, columns(h)],
            dst_ref=kvbuf.at[h, which, r],
            send_sem=kv_send.at[which, h],
            recv_sem=kv_recv.at[which, h],
            device_id={"blk": lax.rem(b + r, blk)},
            device_id_type=MESH,
        )

    def q_copy(source, h, j, way):
        target = t + 1 if way == RIGHT else t - 1
        return pltpu.make_async_remote_copy(
            src_ref=source,
            dst_ref=qbuf.at[h, j],
            send_sem=q_send.at[way, h, j],
            recv_sem=q_recv.at[h, j],
            device_id={"team": target},
            device_id_type=MESH,
        )

    def o_copy(h, j, way):
        target = t + 1 if way == RIGHT else t - 1
        return (
            pltpu.make_async_remote_copy(
                src_ref=o_out.at[way, h, j],
                dst_ref=o_in.at[way, h, j],
                send_sem=o_send.at[way, h, j],
                recv_sem=o_recv.at[way, h, j],
                device_id={"team": target},
                device_id_type=MESH,
            ),
            pltpu.make_async_remote_copy(
                src_ref=s_out.at[way, h, j],
                dst_ref=s_in.at[way, h, j],
                send_sem=s_send.at[way, h, j],
                recv_sem=s_recv.at[way, h, j],
                device_id={"team": target},
                device_id_type=MESH,
            ),
        )

    def send_kv(h):
        for which in range(2):
            @pl.loop(1, blk)
            def _(r):
                kv_copy(h, which, r).start()

    def send_own_q(h):
        @pl.when(t > 0)
        def _():
            q_copy(q_ref.at[:, columns(h)], h, t, LEFT).start()

        @pl.when(t < last)
        def _():
            q_copy(q_ref.at[:, columns(h)], h, t, RIGHT).start()

    def wait_here(ref, semaphore):
        pltpu.make_async_copy(ref, ref, semaphore).wait()

    def relay_q(h, distance):
        @pl.when(t + distance <= last)
        def _():
            j = t + distance
            wait_here(qbuf.at[h, j], q_recv.at[h, j])

            @pl.when(t > 0)
            def _():
                q_copy(qbuf.at[h, j], h, j, LEFT).start()

        @pl.when(t - distance >= 0)
        def _():
            j = t - distance
            wait_here(qbuf.at[h, j], q_recv.at[h, j])

            @pl.when(t < last)
            def _():
                q_copy(qbuf.at[h, j], h, j, RIGHT).start()

    group = math.gcd(blk, 4)
    groups = blk // group

    def attend(h):
        qbuf[h, t] = q_ref[:, columns(h)]
        kvbuf[h, 0, 0] = k_ref[:, columns(h)]
        kvbuf[h, 1, 0] = v_ref[:, columns(h)]
        queries = qbuf[h].reshape(team * rows, HEAD_DIM)
        for which in range(2):
            if blk > 1:
                wait_here(kvbuf.at[h, which, pl.ds(1, blk - 1)], kv_recv.at[which, h])

        def scores_of(c):
            keys = kvbuf[h, 0, pl.ds(c * group, group)].reshape(group * rows, HEAD_DIM)
            return lax.dot_general(
                keys, queries, (((1,), (1,)), ((), ())), preferred_element_type=jnp.float32
            )

        def weighted(c, weights):
            block = kvbuf[h, 1, pl.ds(c * group, group)].reshape(group * rows, HEAD_DIM)
            return lax.dot_general(
                block, weights.astype(jnp.bfloat16), (((0,), (0,)), ((), ())),
                preferred_element_type=jnp.float32,
            )

        scores = scores_of(0)
        peak = jnp.max(scores, axis=0, keepdims=True) * scale
        weights = jnp.exp2(scores * scale - peak)
        total = jnp.sum(weights, axis=0, keepdims=True)
        summed = weighted(0, weights)

        def more(c, state):
            peak, total, summed = state
            scores = scores_of(c)
            higher = jnp.maximum(peak, jnp.max(scores, axis=0, keepdims=True) * scale)
            rescale = jnp.exp2(peak - higher)
            weights = jnp.exp2(scores * scale - higher)
            total = total * rescale + jnp.sum(weights, axis=0, keepdims=True)
            summed = summed * rescale + weighted(c, weights)
            return higher, total, summed

        if groups > 1:
            peak, total, summed = lax.fori_loop(1, groups, more, (peak, total, summed))
        attended = summed * (1.0 / total)
        level = peak + jnp.log2(total)
        for j in range(team):
            part_o[h, j] = attended[:, j * rows : (j + 1) * rows]
            part_s[h, j] = level[:, j * rows : (j + 1) * rows]

    def await_partial(h, j, way):
        wait_here(o_in.at[way, h, j], o_recv.at[way, h, j])
        wait_here(s_in.at[way, h, j], s_recv.at[way, h, j])

    def pass_on(h, way):
        first, stop = (t + 1, team) if way == RIGHT else (0, t)
        is_source = t == 0 if way == RIGHT else t == last

        @pl.loop(first, stop)
        def _(j):
            @pl.when(is_source)
            def _():
                o_out[way, h, j] = part_o[h, j].astype(jnp.bfloat16)
                s_out[way, h, j] = part_s[h, j]

            @pl.when(jnp.logical_not(is_source))
            def _():
                await_partial(h, j, way)
                o, s = merge(
                    part_o[h, j], part_s[h, j],
                    o_in[way, h, j].astype(jnp.float32), s_in[way, h, j],
                )
                o_out[way, h, j] = o.astype(jnp.bfloat16)
                s_out[way, h, j] = s

            for copy in o_copy(h, j, way):
                copy.start()

    def finish(h):
        for way, present in ((RIGHT, t > 0), (LEFT, t < last)):
            @pl.when(present)
            def _():
                await_partial(h, t, way)
                o, s = merge(
                    part_o[h, t], part_s[h, t],
                    o_in[way, h, t].astype(jnp.float32), s_in[way, h, t],
                )
                part_o[h, t] = o
                part_s[h, t] = s

        out_ref[:, columns(h)] = part_o[h, t].T.astype(out_ref.dtype)

    def guarded(h, action):
        @pl.when(jnp.logical_and(h >= 0, h < heads))
        def _():
            action(h)

    @pl.loop(0, heads + 2 * last)
    def _(step):
        @pl.when(step < heads)
        def _():
            send_own_q(step)
            send_kv(step)

        for distance in range(1, team):
            guarded(step - distance, functools.partial(relay_q, distance=distance))
        now = step - last
        guarded(now, attend)
        guarded(now - t, functools.partial(pass_on, way=RIGHT))
        guarded(now - (last - t), functools.partial(pass_on, way=LEFT))
        guarded(now - last, finish)

    @pl.loop(0, heads)
    def _(h):
        if blk > 1:
            for which in range(2):
                wait_here(kvbuf.at[h, which, pl.ds(1, blk - 1)], kv_send.at[which, h])

        @pl.when(t > 0)
        def _():
            @pl.loop(t, team)
            def _(j):
                wait_here(qbuf.at[h, j], q_send.at[LEFT, h, j])

            @pl.loop(0, t)
            def _(j):
                wait_here(o_out.at[LEFT, h, j], o_send.at[LEFT, h, j])
                wait_here(s_out.at[LEFT, h, j], s_send.at[LEFT, h, j])

        @pl.when(t < last)
        def _():
            @pl.loop(0, t + 1)
            def _(j):
                wait_here(qbuf.at[h, j], q_send.at[RIGHT, h, j])

            @pl.loop(t + 1, team)
            def _(j):
                wait_here(o_out.at[RIGHT, h, j], o_send.at[RIGHT, h, j])
                wait_here(s_out.at[RIGHT, h, j], s_send.at[RIGHT, h, j])


def on_device(team, blk, query, keys, values):
    rows, width = query.shape
    heads = width // HEAD_DIM
    dma = pltpu.SemaphoreType.DMA
    bf16, f32 = jnp.bfloat16, jnp.float32
    return pl.pallas_call(
        functools.partial(kernel, team, blk),
        out_shape=jax.ShapeDtypeStruct((rows, width), query.dtype),
        in_specs=[pl.BlockSpec(memory_space=pltpu.VMEM)] * 3,
        out_specs=pl.BlockSpec(memory_space=pltpu.VMEM),
        scratch_shapes=[
            pltpu.VMEM((heads, team, rows, HEAD_DIM), bf16),
            pltpu.VMEM((heads, 2, blk, rows, HEAD_DIM), bf16),
            pltpu.VMEM((heads, team, HEAD_DIM, rows), f32),
            pltpu.VMEM((heads, team, 1, rows), f32),
            pltpu.VMEM((2, heads, team, HEAD_DIM, rows), bf16),
            pltpu.VMEM((2, heads, team, 1, rows), f32),
            pltpu.VMEM((2, heads, team, HEAD_DIM, rows), bf16),
            pltpu.VMEM((2, heads, team, 1, rows), f32),
            dma((heads, team)),
            dma((2, heads, team)),
            dma((2, heads)),
            dma((2, heads)),
            dma((2, heads, team)),
            dma((2, heads, team)),
            dma((2, heads, team)),
            dma((2, heads, team)),
        ],
        compiler_params=pltpu.CompilerParams(
            collective_id=0, has_side_effects=True, vmem_limit_bytes=60 * 1024 * 1024
        ),
    )(query, keys, values)


def solution(mesh):
    placed = P(("team", "blk"), "head")
    return jax.shard_map(
        functools.partial(on_device, mesh.shape["team"], mesh.shape["blk"]),
        mesh=mesh, in_specs=(placed,) * 3, out_specs=placed, check_vma=False,
    )
```

```python
import functools
import math

import jax
import jax.numpy as jnp
from jax import lax
from jax.experimental import pallas as pl
from jax.experimental.pallas import tpu as pltpu
from jax.sharding import PartitionSpec as P

HEAD_DIM = 128
MESH = pl.DeviceIdType.MESH
RIGHT, LEFT = 0, 1
QUERY_LAG = 2
PARTIAL_LAG = 2


def merge(o1, s1, o2, s2):
    top = jnp.maximum(s1, s2)
    a1 = jnp.exp2(s1 - top)
    a2 = jnp.exp2(s2 - top)
    total = a1 + a2
    inverse = 1.0 / total
    return o1 * (a1 * inverse) + o2 * (a2 * inverse), top + jnp.log2(total)


def kernel(
    team, blk, q_ref, k_ref, v_ref, out_ref,
    qbuf, kvbuf, part_o, part_s, o_in, s_in, o_out, s_out, pair_size,
    local, q_recv, q_send, kv_recv, kv_send, o_recv, o_send, s_send,
):
    rows = q_ref.shape[0]
    heads = q_ref.shape[1] // HEAD_DIM
    scale = math.log2(math.e) / math.sqrt(HEAD_DIM)
    t = lax.axis_index("team")
    b = lax.axis_index("blk")
    last = team - 1

    def columns(h):
        return pl.ds(pl.multiple_of(h * HEAD_DIM, HEAD_DIM), HEAD_DIM)

    def wait_here(ref, semaphore):
        pltpu.make_async_copy(ref, ref, semaphore).wait()

    def load(h):
        return (
            pltpu.make_async_copy(q_ref.at[:, columns(h)], qbuf.at[h, t], local.at[0]),
            pltpu.make_async_copy(k_ref.at[:, columns(h)], kvbuf.at[h, 0, 0], local.at[1]),
            pltpu.make_async_copy(v_ref.at[:, columns(h)], kvbuf.at[h, 1, 0], local.at[2]),
        )

    @pl.loop(0, heads)
    def _(h):
        for copy in load(h):
            copy.start()

    barrier = pltpu.get_barrier_semaphore()

    @pl.loop(1, blk)
    def _(r):
        pl.semaphore_signal(
            barrier, inc=1, device_id={"blk": lax.rem(b + r, blk)}, device_id_type=MESH
        )

    @pl.when(t > 0)
    def _():
        pl.semaphore_signal(barrier, inc=1, device_id={"team": t - 1}, device_id_type=MESH)

    @pl.when(t < last)
    def _():
        pl.semaphore_signal(barrier, inc=1, device_id={"team": t + 1}, device_id_type=MESH)

    ends = jnp.where(t > 0, 1, 0) + jnp.where(t < last, 1, 0)
    pl.semaphore_wait(barrier, blk - 1 + ends)
    wait_here(qbuf.at[:, t], local.at[0])
    wait_here(kvbuf.at[:, 0, 0], local.at[1])
    wait_here(kvbuf.at[:, 1, 0], local.at[2])

    def kv_copy(h, which, r):
        return pltpu.make_async_remote_copy(
            src_ref=kvbuf.at[h, which, 0],
            dst_ref=kvbuf.at[h, which, r],
            send_sem=kv_send.at[0],
            recv_sem=kv_recv.at[h],
            device_id={"blk": lax.rem(b + r, blk)},
            device_id_type=MESH,
        )

    def q_copy(source, h, j, way):
        target = t + 1 if way == RIGHT else t - 1
        return pltpu.make_async_remote_copy(
            src_ref=source,
            dst_ref=qbuf.at[h, j],
            send_sem=q_send.at[way, j],
            recv_sem=q_recv.at[h, j],
            device_id={"team": target},
            device_id_type=MESH,
        )

    def o_copy(h, j, way):
        target = t + 1 if way == RIGHT else t - 1
        return (
            pltpu.make_async_remote_copy(
                src_ref=o_out.at[way, h, j],
                dst_ref=o_in.at[h, j + 1 - way],
                send_sem=o_send.at[way, j],
                recv_sem=o_recv.at[h, j + 1 - way],
                device_id={"team": target},
                device_id_type=MESH,
            ),
            pltpu.make_async_remote_copy(
                src_ref=s_out.at[way, h, j],
                dst_ref=s_in.at[h, j + 1 - way],
                send_sem=s_send.at[way, j],
                recv_sem=o_recv.at[h, j + 1 - way],
                device_id={"team": target},
                device_id_type=MESH,
            ),
        )

    def send_kv(h):
        for which in range(2):
            @pl.loop(1, blk)
            def _(r):
                kv_copy(h, which, r).start()

    def send_own_q(h):
        @pl.when(t > 0)
        def _():
            q_copy(qbuf.at[h, t], h, t, LEFT).start()

        @pl.when(t < last)
        def _():
            q_copy(qbuf.at[h, t], h, t, RIGHT).start()

    def relay_q(h, distance):
        @pl.when(t + distance <= last)
        def _():
            j = t + distance
            wait_here(qbuf.at[h, j], q_recv.at[h, j])

            @pl.when(t > 0)
            def _():
                q_copy(qbuf.at[h, j], h, j, LEFT).start()

        @pl.when(t - distance >= 0)
        def _():
            j = t - distance
            wait_here(qbuf.at[h, j], q_recv.at[h, j])

            @pl.when(t < last)
            def _():
                q_copy(qbuf.at[h, j], h, j, RIGHT).start()

    group = math.gcd(blk, 4)
    groups = blk // group

    def attend(h):
        queries = qbuf[h].reshape(team * rows, HEAD_DIM)
        if blk > 1:
            wait_here(kvbuf.at[h, :, pl.ds(1, blk - 1)], kv_recv.at[h])

        def scores_of(c):
            keys = kvbuf[h, 0, pl.ds(c * group, group)].reshape(group * rows, HEAD_DIM)
            return lax.dot_general(
                keys, queries, (((1,), (1,)), ((), ())), preferred_element_type=jnp.float32
            )

        def weighted(c, weights):
            block = kvbuf[h, 1, pl.ds(c * group, group)].reshape(group * rows, HEAD_DIM)
            return lax.dot_general(
                block, weights.astype(jnp.bfloat16), (((0,), (0,)), ((), ())),
                preferred_element_type=jnp.float32,
            )

        scores = scores_of(0)
        peak = jnp.max(scores, axis=0, keepdims=True) * scale
        weights = jnp.exp2(scores * scale - peak)
        total = jnp.sum(weights, axis=0, keepdims=True)
        summed = weighted(0, weights)

        def more(c, state):
            peak, total, summed = state
            scores = scores_of(c)
            higher = jnp.maximum(peak, jnp.max(scores, axis=0, keepdims=True) * scale)
            rescale = jnp.exp2(peak - higher)
            weights = jnp.exp2(scores * scale - higher)
            total = total * rescale + jnp.sum(weights, axis=0, keepdims=True)
            summed = summed * rescale + weighted(c, weights)
            return higher, total, summed

        if groups > 1:
            peak, total, summed = lax.fori_loop(1, groups, more, (peak, total, summed))
        attended = summed * (1.0 / total)
        level = peak + jnp.log2(total)
        for j in range(team):
            part_o[h, j] = attended[:, j * rows : (j + 1) * rows]
            part_s[h, j] = level[:, j * rows : (j + 1) * rows]

    def await_partial(h, j, way):
        wait_here(pair_size, o_recv.at[h, j + 1 - way])

    def pass_on(h, way):
        first, stop = (t + 1, team) if way == RIGHT else (0, t)
        is_source = t == 0 if way == RIGHT else t == last

        @pl.loop(first, stop)
        def _(index):
            j = stop - 1 - (index - first) if way == RIGHT else index

            @pl.when(is_source)
            def _():
                o_out[way, h, j] = part_o[h, j].astype(jnp.bfloat16)
                s_out[way, h, j] = part_s[h, j]

            @pl.when(jnp.logical_not(is_source))
            def _():
                await_partial(h, j, way)
                o, s = merge(
                    part_o[h, j], part_s[h, j],
                    o_in[h, j + 1 - way].astype(jnp.float32), s_in[h, j + 1 - way],
                )
                o_out[way, h, j] = o.astype(jnp.bfloat16)
                s_out[way, h, j] = s

            for copy in o_copy(h, j, way):
                copy.start()

    def finish(h):
        for way, present in ((RIGHT, t > 0), (LEFT, t < last)):
            @pl.when(present)
            def _():
                await_partial(h, t, way)
                o, s = merge(
                    part_o[h, t], part_s[h, t],
                    o_in[h, t + 1 - way].astype(jnp.float32), s_in[h, t + 1 - way],
                )
                part_o[h, t] = o
                part_s[h, t] = s

        out_ref[:, columns(h)] = part_o[h, t].T.astype(out_ref.dtype)

    def guarded(h, action):
        @pl.when(jnp.logical_and(h >= 0, h < heads))
        def _():
            action(h)

    @pl.loop(0, heads + (QUERY_LAG + PARTIAL_LAG) * last)
    def _(step):
        @pl.when(step < heads)
        def _():
            send_own_q(step)
            send_kv(step)

        for distance in range(1, team):
            guarded(
                step - QUERY_LAG * distance, functools.partial(relay_q, distance=distance)
            )
        now = step - QUERY_LAG * last
        guarded(now, attend)
        guarded(now - PARTIAL_LAG * t, functools.partial(pass_on, way=RIGHT))
        guarded(now - PARTIAL_LAG * (last - t), functools.partial(pass_on, way=LEFT))
        guarded(now - PARTIAL_LAG * last, finish)

    if blk > 1:
        wait_here(kvbuf.at[:, :, pl.ds(1, blk - 1)], kv_send.at[0])

    def drain(way, first_q, stop_q, first_o, stop_o):
        @pl.loop(first_q, stop_q)
        def _(j):
            wait_here(qbuf.at[:, j], q_send.at[way, j])

        @pl.loop(first_o, stop_o)
        def _(j):
            wait_here(o_out.at[way, :, j], o_send.at[way, j])
            wait_here(s_out.at[way, :, j], s_send.at[way, j])

    @pl.when(t > 0)
    def _():
        drain(LEFT, t, team, 0, t)

    @pl.when(t < last)
    def _():
        drain(RIGHT, 0, t + 1, t + 1, team)


def on_device(team, blk, query, keys, values):
    rows, width = query.shape
    heads = width // HEAD_DIM
    dma = pltpu.SemaphoreType.DMA
    bf16, f32 = jnp.bfloat16, jnp.float32
    return pl.pallas_call(
        functools.partial(kernel, team, blk),
        out_shape=jax.ShapeDtypeStruct((rows, width), query.dtype),
        in_specs=[pl.BlockSpec(memory_space=pl.ANY)] * 3,
        out_specs=pl.BlockSpec(memory_space=pltpu.VMEM),
        scratch_shapes=[
            pltpu.VMEM((heads, team, rows, HEAD_DIM), bf16),
            pltpu.VMEM((heads, 2, blk, rows, HEAD_DIM), bf16),
            pltpu.VMEM((heads, team, HEAD_DIM, rows), f32),
            pltpu.VMEM((heads, team, 1, rows), f32),
            pltpu.VMEM((heads, team + 1, HEAD_DIM, rows), bf16),
            pltpu.VMEM((heads, team + 1, 1, rows), f32),
            pltpu.VMEM((2, heads, team, HEAD_DIM, rows), bf16),
            pltpu.VMEM((2, heads, team, 1, rows), f32),
            pltpu.VMEM((HEAD_DIM // 2 + 1, 1, rows), f32),
            dma((3,)),
            dma((heads, team)),
            dma((2, team)),
            dma((heads,)),
            dma((1,)),
            dma((heads, team + 1)),
            dma((2, team)),
            dma((2, team)),
        ],
        compiler_params=pltpu.CompilerParams(
            collective_id=0, has_side_effects=True, vmem_limit_bytes=60 * 1024 * 1024
        ),
    )(query, keys, values)


def solution(mesh):
    placed = P(("team", "blk"), "head")
    return jax.shard_map(
        functools.partial(on_device, mesh.shape["team"], mesh.shape["blk"]),
        mesh=mesh, in_specs=(placed,) * 3, out_specs=placed, check_vma=False,
    )
```

```python
import functools
import math

import jax
import jax.numpy as jnp
from jax import lax
from jax.experimental import pallas as pl
from jax.experimental.pallas import tpu as pltpu
from jax.sharding import PartitionSpec as P

HEAD_DIM = 128
MESH = pl.DeviceIdType.MESH
RIGHT, LEFT = 0, 1
QUERY_LAG = 2
PARTIAL_LAG = 2


def merge(o1, s1, o2, s2):
    top = jnp.maximum(s1, s2)
    a1 = jnp.exp2(s1 - top)
    a2 = jnp.exp2(s2 - top)
    total = a1 + a2
    inverse = 1.0 / total
    return o1 * (a1 * inverse) + o2 * (a2 * inverse), top + jnp.log2(total)


def kernel(
    team, blk, q_ref, k_ref, v_ref, out_ref,
    qbuf, kvbuf, part_o, part_s, o_in, s_in, o_out, s_out, pair_size,
    local, q_recv, q_send, kv_recv, kv_send, o_recv, o_send, s_send,
):
    rows = q_ref.shape[0]
    heads = q_ref.shape[1] // HEAD_DIM
    scale = math.log2(math.e) / math.sqrt(HEAD_DIM)
    t = lax.axis_index("team")
    b = lax.axis_index("blk")
    last = team - 1

    def columns(h):
        return pl.ds(pl.multiple_of(h * HEAD_DIM, HEAD_DIM), HEAD_DIM)

    def wait_here(ref, semaphore):
        pltpu.make_async_copy(ref, ref, semaphore).wait()

    def load(h):
        return (
            pltpu.make_async_copy(q_ref.at[:, columns(h)], qbuf.at[h, t], local.at[0]),
            pltpu.make_async_copy(k_ref.at[:, columns(h)], kvbuf.at[h, 0, 0], local.at[1]),
            pltpu.make_async_copy(v_ref.at[:, columns(h)], kvbuf.at[h, 1, 0], local.at[2]),
        )

    @pl.loop(0, heads)
    def _(h):
        for copy in load(h):
            copy.start()

    barrier = pltpu.get_barrier_semaphore()

    @pl.loop(1, blk)
    def _(r):
        pl.semaphore_signal(
            barrier, inc=1, device_id={"blk": lax.rem(b + r, blk)}, device_id_type=MESH
        )

    @pl.when(t > 0)
    def _():
        pl.semaphore_signal(barrier, inc=1, device_id={"team": t - 1}, device_id_type=MESH)

    @pl.when(t < last)
    def _():
        pl.semaphore_signal(barrier, inc=1, device_id={"team": t + 1}, device_id_type=MESH)

    ends = jnp.where(t > 0, 1, 0) + jnp.where(t < last, 1, 0)
    pl.semaphore_wait(barrier, blk - 1 + ends)
    wait_here(qbuf.at[:, t], local.at[0])
    wait_here(kvbuf.at[:, 0, 0], local.at[1])
    wait_here(kvbuf.at[:, 1, 0], local.at[2])

    def kv_copy(h, r):
        return pltpu.make_async_remote_copy(
            src_ref=kvbuf.at[h, :, 0],
            dst_ref=kvbuf.at[h, :, r],
            send_sem=kv_send.at[0],
            recv_sem=kv_recv.at[h],
            device_id={"blk": lax.rem(b + r, blk)},
            device_id_type=MESH,
        )

    def q_copy(source, h, j, way):
        target = t + 1 if way == RIGHT else t - 1
        return pltpu.make_async_remote_copy(
            src_ref=source,
            dst_ref=qbuf.at[h, j],
            send_sem=q_send.at[way, j],
            recv_sem=q_recv.at[h, j],
            device_id={"team": target},
            device_id_type=MESH,
        )

    def o_copy(h, j, way):
        target = t + 1 if way == RIGHT else t - 1
        return (
            pltpu.make_async_remote_copy(
                src_ref=o_out.at[way, h, j],
                dst_ref=o_in.at[h, j + 1 - way],
                send_sem=o_send.at[way, j],
                recv_sem=o_recv.at[h, j + 1 - way],
                device_id={"team": target},
                device_id_type=MESH,
            ),
            pltpu.make_async_remote_copy(
                src_ref=s_out.at[way, h, j],
                dst_ref=s_in.at[h, j + 1 - way],
                send_sem=s_send.at[way, j],
                recv_sem=o_recv.at[h, j + 1 - way],
                device_id={"team": target},
                device_id_type=MESH,
            ),
        )

    def send_kv(h):
        @pl.loop(1, blk)
        def _(r):
            kv_copy(h, r).start()

    def send_own_q(h):
        @pl.when(t > 0)
        def _():
            q_copy(qbuf.at[h, t], h, t, LEFT).start()

        @pl.when(t < last)
        def _():
            q_copy(qbuf.at[h, t], h, t, RIGHT).start()

    def relay_q(h, distance):
        @pl.when(t + distance <= last)
        def _():
            j = t + distance
            wait_here(qbuf.at[h, j], q_recv.at[h, j])

            @pl.when(t > 0)
            def _():
                q_copy(qbuf.at[h, j], h, j, LEFT).start()

        @pl.when(t - distance >= 0)
        def _():
            j = t - distance
            wait_here(qbuf.at[h, j], q_recv.at[h, j])

            @pl.when(t < last)
            def _():
                q_copy(qbuf.at[h, j], h, j, RIGHT).start()

    group = math.gcd(blk, 4)
    groups = blk // group

    def attend(h):
        queries = qbuf[h].reshape(team * rows, HEAD_DIM)
        if blk > 1:
            wait_here(kvbuf.at[h, :, pl.ds(1, blk - 1)], kv_recv.at[h])

        def scores_of(c):
            keys = kvbuf[h, 0, pl.ds(c * group, group)].reshape(group * rows, HEAD_DIM)
            return lax.dot_general(
                keys, queries, (((1,), (1,)), ((), ())), preferred_element_type=jnp.float32
            )

        def weighted(c, weights):
            block = kvbuf[h, 1, pl.ds(c * group, group)].reshape(group * rows, HEAD_DIM)
            return lax.dot_general(
                block, weights.astype(jnp.bfloat16), (((0,), (0,)), ((), ())),
                preferred_element_type=jnp.float32,
            )

        scores = scores_of(0)
        peak = jnp.max(scores, axis=0, keepdims=True) * scale
        weights = jnp.exp2(scores * scale - peak)
        total = jnp.sum(weights, axis=0, keepdims=True)
        summed = weighted(0, weights)

        def more(c, state):
            peak, total, summed = state
            scores = scores_of(c)
            higher = jnp.maximum(peak, jnp.max(scores, axis=0, keepdims=True) * scale)
            rescale = jnp.exp2(peak - higher)
            weights = jnp.exp2(scores * scale - higher)
            total = total * rescale + jnp.sum(weights, axis=0, keepdims=True)
            summed = summed * rescale + weighted(c, weights)
            return higher, total, summed

        if groups > 1:
            peak, total, summed = lax.fori_loop(1, groups, more, (peak, total, summed))
        attended = summed * (1.0 / total)
        level = peak + jnp.log2(total)
        for j in range(team):
            part_o[h, j] = attended[:, j * rows : (j + 1) * rows]
            part_s[h, j] = level[:, j * rows : (j + 1) * rows]

    def await_partial(h, j, way):
        wait_here(pair_size, o_recv.at[h, j + 1 - way])

    def pass_on(h, way):
        first, stop = (t + 1, team) if way == RIGHT else (0, t)
        is_source = t == 0 if way == RIGHT else t == last

        @pl.loop(first, stop)
        def _(index):
            j = stop - 1 - (index - first) if way == RIGHT else index

            @pl.when(is_source)
            def _():
                o_out[way, h, j] = part_o[h, j].astype(jnp.bfloat16)
                s_out[way, h, j] = part_s[h, j]

            @pl.when(jnp.logical_not(is_source))
            def _():
                await_partial(h, j, way)
                o, s = merge(
                    part_o[h, j], part_s[h, j],
                    o_in[h, j + 1 - way].astype(jnp.float32), s_in[h, j + 1 - way],
                )
                o_out[way, h, j] = o.astype(jnp.bfloat16)
                s_out[way, h, j] = s

            for copy in o_copy(h, j, way):
                copy.start()

    def finish(h):
        for way, present in ((RIGHT, t > 0), (LEFT, t < last)):
            @pl.when(present)
            def _():
                await_partial(h, t, way)
                o, s = merge(
                    part_o[h, t], part_s[h, t],
                    o_in[h, t + 1 - way].astype(jnp.float32), s_in[h, t + 1 - way],
                )
                part_o[h, t] = o
                part_s[h, t] = s

        out_ref[:, columns(h)] = part_o[h, t].T.astype(out_ref.dtype)

    def guarded(h, action):
        @pl.when(jnp.logical_and(h >= 0, h < heads))
        def _():
            action(h)

    @pl.loop(0, heads + (QUERY_LAG + PARTIAL_LAG) * last)
    def _(step):
        @pl.when(step < heads)
        def _():
            send_own_q(step)
            send_kv(step)

        for distance in range(1, team):
            guarded(
                step - QUERY_LAG * distance, functools.partial(relay_q, distance=distance)
            )
        now = step - QUERY_LAG * last
        guarded(now, attend)
        guarded(now - PARTIAL_LAG * t, functools.partial(pass_on, way=RIGHT))
        guarded(now - PARTIAL_LAG * (last - t), functools.partial(pass_on, way=LEFT))
        guarded(now - PARTIAL_LAG * last, finish)

    if blk > 1:
        wait_here(kvbuf.at[:, :, pl.ds(1, blk - 1)], kv_send.at[0])

    def drain(way, first_q, stop_q, first_o, stop_o):
        @pl.loop(first_q, stop_q)
        def _(j):
            wait_here(qbuf.at[:, j], q_send.at[way, j])

        @pl.loop(first_o, stop_o)
        def _(j):
            wait_here(o_out.at[way, :, j], o_send.at[way, j])
            wait_here(s_out.at[way, :, j], s_send.at[way, j])

    @pl.when(t > 0)
    def _():
        drain(LEFT, t, team, 0, t)

    @pl.when(t < last)
    def _():
        drain(RIGHT, 0, t + 1, t + 1, team)


def on_device(team, blk, query, keys, values):
    rows, width = query.shape
    heads = width // HEAD_DIM
    dma = pltpu.SemaphoreType.DMA
    bf16, f32 = jnp.bfloat16, jnp.float32
    return pl.pallas_call(
        functools.partial(kernel, team, blk),
        out_shape=jax.ShapeDtypeStruct((rows, width), query.dtype),
        in_specs=[pl.BlockSpec(memory_space=pl.ANY)] * 3,
        out_specs=pl.BlockSpec(memory_space=pltpu.VMEM),
        scratch_shapes=[
            pltpu.VMEM((heads, team, rows, HEAD_DIM), bf16),
            pltpu.VMEM((heads, 2, blk, rows, HEAD_DIM), bf16),
            pltpu.VMEM((heads, team, HEAD_DIM, rows), f32),
            pltpu.VMEM((heads, team, 1, rows), f32),
            pltpu.VMEM((heads, team + 1, HEAD_DIM, rows), bf16),
            pltpu.VMEM((heads, team + 1, 1, rows), f32),
            pltpu.VMEM((2, heads, team, HEAD_DIM, rows), bf16),
            pltpu.VMEM((2, heads, team, 1, rows), f32),
            pltpu.VMEM((HEAD_DIM // 2 + 1, 1, rows), f32),
            dma((3,)),
            dma((heads, team)),
            dma((2, team)),
            dma((heads,)),
            dma((1,)),
            dma((heads, team + 1)),
            dma((2, team)),
            dma((2, team)),
        ],
        compiler_params=pltpu.CompilerParams(
            collective_id=0, has_side_effects=True, vmem_limit_bytes=60 * 1024 * 1024
        ),
    )(query, keys, values)


def solution(mesh):
    placed = P(("team", "blk"), "head")
    return jax.shard_map(
        functools.partial(on_device, mesh.shape["team"], mesh.shape["blk"]),
        mesh=mesh, in_specs=(placed,) * 3, out_specs=placed, check_vma=False,
    )
```
